32 devices in a mesh: pipe: 2 (over core), row: 4 (over z), rep: 4 (over y, x).
Axes of the slice: x: 2, y: 2, z: 4, core: 2. Of those that a mesh axis runs over, the one named last changes fastest.
Arguments:
- features: bfloat16 [1, 4096, 256], P(None, ('pipe', 'row')), may hold values from -6 to 6
- tile_src: int32 [8, 4, 2, 12], P(('pipe', 'row'), 'rep'), may hold values from 0 to 7
- tile_dst: int32 [8, 4, 2, 12], P(('pipe', 'row'), 'rep'), may hold values from 0 to 7
- tile_count: int32 [8, 4, 2], P(('pipe', 'row'), 'rep'), may hold values from 1 to 12, as said below
- edge_dst: int32 [8, 4, 2, 12, 256], P(('pipe', 'row'), 'rep'), may hold values from 0 to 63
- edge_src: int32 [8, 4, 2, 12, 256], P(('pipe', 'row'), 'rep'), may hold values from 0 to 63
- edge_weight: float32 [8, 4, 2, 12, 256], P(('pipe', 'row'), 'rep'), may hold values from 0.25 to 4
- w_msg: bfloat16 [2, 256, 256], replicated, may hold values from -0.375 to 0.375
- w_self: bfloat16 [2, 256, 256], replicated, may hold values from -0.375 to 0.375
- w_mid: bfloat16 [2, 256, 256], replicated, may hold values from -0.375 to 0.375
- w_out: bfloat16 [2, 256, 256], replicated, may hold values from -0.375 to 0.375
- gain: float32 [2, 256], replicated, may hold values from 0.1 to 1.9
Outputs:
- hidden: bfloat16 [2, 1, 4096, 256], P(None, None, ('pipe', 'row'))
The draws below stay inside these ranges and needn't reach their ends.
Inputs may be any that keep to these rules, and one draw needn't show every extreme that they name: `tile_count`: every entry is at least 1 and at most 12; for every row block and every index of rep, some section has exactly 12 live slots.
All inputs are finite; a program needn't handle non-finite values.
Results may differ from the reference program's by a relative error of at most 0.0054.
Values may be sent and summed in bfloat16 or wider, within the bound.
A program may use at most 64 MiB of HBM per device.

```python
import math
import jax
import jax.numpy as jnp
from jax import lax

F = 256
BS = 64
LAYERS = 2
NR = 512
MB = 1
KS = 12
EB = 256
NB = 8
NG = 8
SJ = 2
NN = 4096
N_REP = 4


def draw_tile_count(key, part):
    first_key, second_key = jax.random.split(jax.random.fold_in(key, 11))
    base = jax.random.randint(first_key, (NG, N_REP, SJ), 1, KS + 1)
    picked = jax.random.randint(second_key, (NG, N_REP, 1), 0, SJ)
    full = jnp.arange(SJ)[None, None, :] == picked
    return jnp.where(full, KS, base).astype(jnp.int32)


def plant(values, key, smallest, high):
    extent = values.shape
    index_at = [jax.random.randint(jax.random.fold_in(key, axis), (), 0, extent[axis]) for axis in range(len(extent))]
    values = values.at[tuple(index_at)].set(smallest)
    longest = extent.index(max(extent))
    index_at[longest] = (index_at[longest] + 1) % extent[longest]
    return values.at[tuple(index_at)].set(high)


def levels(key, extent, shards, smallest, top_value):
    loudness = 1.0
    for dim, shards_of in shards:
        steps = jax.random.uniform(jax.random.fold_in(jax.random.fold_in(key, 6), dim), (shards_of,), jnp.float32, smallest / len(shards), top_value / len(shards))
        loudness = loudness * jnp.repeat(jnp.exp(steps), extent[dim] // shards_of).reshape((-1,) + (1,) * (len(extent) - 1 - dim))
    return loudness


def bell_draw(stream_key, shape, width, limit, shards=(), held_as=jnp.bfloat16):
    level = levels(stream_key, shape, shards, -0.22, 0.18) if shards else 1.0
    values = jax.random.normal(stream_key, shape, jnp.float32) * width * level
    return jnp.minimum(jnp.maximum(values, -limit), limit).astype(held_as)


def setup_inputs(seed: int = 0) -> dict:
    seeds = jax.random.split(jax.random.key(seed), 13)
    return {
        "features": bell_draw(seeds[0], (MB, NN, F), 1.0, 6.0, ((1, 8),)),
        "tile_src": plant(jax.random.randint(seeds[1], (NG, N_REP, SJ, KS), 0, NB), jax.random.fold_in(seeds[1], 1), 0, NB - 1).astype(jnp.int32),
        "tile_dst": plant(jax.random.randint(seeds[2], (NG, N_REP, SJ, KS), 0, NB), jax.random.fold_in(seeds[2], 1), 0, NB - 1).astype(jnp.int32),
        "tile_count": draw_tile_count(jax.random.fold_in(seeds[12], 71), 0),
        "edge_dst": plant(jax.random.randint(seeds[4], (NG, N_REP, SJ, KS, EB), 0, BS), jax.random.fold_in(seeds[4], 1), 0, BS - 1).astype(jnp.int32),
        "edge_src": plant(jax.random.randint(seeds[5], (NG, N_REP, SJ, KS, EB), 0, BS), jax.random.fold_in(seeds[5], 1), 0, BS - 1).astype(jnp.int32),
        "edge_weight": jnp.clip(jnp.exp(math.log(4.0) - 2.7725887 * jax.random.uniform(seeds[6], (NG, N_REP, SJ, KS, EB), jnp.float32) ** levels(seeds[6], (NG, N_REP, SJ, KS, EB), ((0, 8), (1, 4)), -0.2, 0.2)), 0.25, 4.0),
        "w_msg": bell_draw(seeds[7], (LAYERS, F, F), F ** -0.5, 0.375),
        "w_self": bell_draw(seeds[8], (LAYERS, F, F), F ** -0.5, 0.375),
        "w_mid": bell_draw(seeds[9], (LAYERS, F, F), F ** -0.5, 0.375),
        "w_out": bell_draw(seeds[10], (LAYERS, F, F), F ** -0.5, 0.375),
        "gain": jnp.clip(1.0 + 0.18 * jax.random.normal(seeds[11], (LAYERS, F), jnp.float32), 0.1, 1.9),
    }


def build_tiles(dst, src, weight):
    hot_dst = (dst[..., None] == jnp.arange(BS)).astype(jnp.float32) * weight[..., None]
    hot_src = (src[..., None] == jnp.arange(BS)).astype(jnp.float32)
    made = jnp.einsum('...ea,...eb->...ab', hot_dst, hot_src, precision=lax.Precision.HIGHEST)
    return made.astype(jnp.bfloat16)

def aggregate(y, tile_src, tile_dst, tile_count, edge_dst, edge_src, edge_weight):
    blocks_all = y.reshape(NN // BS, BS, F)
    section_ids = jnp.arange(SJ)[None, :] * N_REP + jnp.arange(N_REP)[:, None]

    def one_row(args):
        src_r, dst_r, count_r, edst_r, esrc_r, ew_r = args
        tiles = build_tiles(edst_r, esrc_r, ew_r).astype(jnp.float32)
        glob = (section_ids[:, :, None] * NB + src_r).astype(jnp.int32)
        picked = blocks_all[glob].astype(jnp.float32)
        prod = jnp.einsum('csktu,cskuf->csktf', tiles, picked, precision=lax.Precision.HIGHEST)
        live = (jnp.arange(KS)[None, None, :] < count_r[:, :, None]).astype(jnp.float32)
        hot = (dst_r[..., None] == jnp.arange(NB)).astype(jnp.float32) * live[..., None]
        summed = jnp.einsum('cskb,csktf->btf', hot, prod, precision=lax.Precision.HIGHEST)
        return summed.reshape(NR, F)
    result = lax.map(one_row, (tile_src, tile_dst, tile_count, edge_dst, edge_src, edge_weight))
    return result.reshape(NN, F)

def update_rows(rows_in, summed, wself, wmid, wout, gain_row):
    stat = lax.optimization_barrier(jnp.mean(summed * summed, axis=-1, keepdims=True))
    normed = summed * lax.rsqrt(stat + 1e-05) * gain_row
    pre = jnp.dot(rows_in, wself, preferred_element_type=jnp.float32) + normed
    first = jax.nn.silu(pre).astype(jnp.bfloat16)
    second = jax.nn.silu(jnp.dot(first, wmid, preferred_element_type=jnp.float32)).astype(jnp.bfloat16)
    return (rows_in.astype(jnp.float32) + jnp.dot(second, wout, preferred_element_type=jnp.float32)).astype(jnp.bfloat16)

def reference(features, tile_src, tile_dst, tile_count, edge_dst, edge_src, edge_weight, w_msg, w_self, w_mid, w_out, gain):
    graph = (tile_src, tile_dst, tile_count, edge_dst, edge_src, edge_weight)
    outputs = []
    for layer in range(LAYERS):
        outputs.append([])
    for event in range(MB):
        state = features[event]
        for layer in range(LAYERS):
            y = jnp.dot(state, w_msg[layer], preferred_element_type=jnp.float32).astype(jnp.bfloat16)
            summed = aggregate(y, *graph)
            state = update_rows(state, summed, w_self[layer], w_mid[layer], w_out[layer], gain[layer])
            outputs[layer].append(state)
    return jnp.stack([jnp.stack(items) for items in outputs])
```

```python
import functools

import jax
import jax.numpy as jnp
from jax import lax
from jax.experimental import pallas as pl
from jax.experimental.pallas import tpu as pltpu
from jax.sharding import PartitionSpec as P

BS = 64
LAYERS = 2
LANES = 128
HALF = 64
MESH = pl.DeviceIdType.MESH


def build_tiles(dst, src, weight):
    hot_dst = (dst[..., None] == jnp.arange(BS)).astype(jnp.float32) * weight[..., None]
    hot_src = (src[..., None] == jnp.arange(BS)).astype(jnp.float32)
    made = jnp.einsum("...ea,...eb->...ab", hot_dst, hot_src, precision=lax.Precision.HIGHEST)
    return made.astype(jnp.bfloat16)


def section_product(source, tiles_now, src_now, hot_now):
    rows, width = source.shape
    blocked = source.reshape(rows // BS, BS, width)
    picked = jnp.take(blocked, src_now, axis=0)
    prod = jnp.einsum("kab,kbf->kaf", tiles_now, picked, preferred_element_type=jnp.float32)
    summed = jnp.einsum("kn,kaf->naf", hot_now, prod, precision=lax.Precision.HIGHEST)
    return summed.reshape(rows, width)


def update_rows(rows_in, summed, wself, wmid, wout, gain_row):
    stat = jnp.mean(summed * summed, axis=-1, keepdims=True)
    normed = summed * lax.rsqrt(stat + 1e-05) * gain_row
    pre = jnp.dot(rows_in, wself, preferred_element_type=jnp.float32) + normed
    first = jax.nn.silu(pre).astype(jnp.bfloat16)
    second = jax.nn.silu(jnp.dot(first, wmid, preferred_element_type=jnp.float32)).astype(
        jnp.bfloat16
    )
    return (
        rows_in.astype(jnp.float32) + jnp.dot(second, wout, preferred_element_type=jnp.float32)
    ).astype(jnp.bfloat16)


def by_sections(
    features,
    tile_src,
    tile_dst,
    tile_count,
    edge_dst,
    edge_src,
    edge_weight,
    w_msg,
    w_self,
    w_mid,
    w_out,
    gain,
):
    events, rows, width = features.shape
    blocks = rows // BS
    slots = tile_src.shape[3]
    rep_count = lax.axis_size("rep")
    my_rep = lax.axis_index("rep")
    quarter = width // rep_count
    tiles = build_tiles(edge_dst[0, 0], edge_src[0, 0], edge_weight[0, 0])
    live_int = (jnp.arange(slots)[None, :] < tile_count[0, 0][:, None]).astype(jnp.int32)
    src_idx = tile_src[0, 0]
    dst_idx = tile_dst[0, 0]
    tiles_all = lax.all_gather(tiles[None], "rep", axis=0, tiled=True)
    index_all = lax.all_gather(
        jnp.stack([src_idx, dst_idx, live_int])[None], "rep", axis=0, tiled=True
    )
    results = []
    for level in range(LAYERS):
        results.append([])
    state = features[0]
    for level in range(LAYERS):
        wmsg = w_msg[level]
        wself = w_self[level]
        wmid = w_mid[level]
        wout = w_out[level]
        gain_row = gain[level]
        y = jnp.dot(state, wmsg, preferred_element_type=jnp.float32).astype(jnp.bfloat16)
        y_share = lax.dynamic_slice_in_dim(y, my_rep * quarter, quarter, 1)
        piece = lax.all_gather(y_share, ("pipe", "row"), axis=0, tiled=True)
        count = piece.shape[0] // rows

        def one_block(i, acc):
            owner_rep = i % rep_count
            section = i // rep_count
            tiles_rep = lax.dynamic_index_in_dim(tiles_all, owner_rep, 0, keepdims=False)
            tiles_now = lax.dynamic_index_in_dim(tiles_rep, section, 0, keepdims=False)
            info_rep = lax.dynamic_index_in_dim(index_all, owner_rep, 0, keepdims=False)
            info = lax.dynamic_index_in_dim(info_rep, section, 1, keepdims=False)
            hot_now = (info[1][:, None] == jnp.arange(blocks)).astype(jnp.float32) * info[2].astype(
                jnp.float32
            )[:, None]
            sub = lax.dynamic_slice_in_dim(piece, i * rows, rows, 0)
            return acc + section_product(sub, tiles_now, info[0], hot_now)

        column_sum = lax.fori_loop(0, count, one_block, jnp.zeros((rows, quarter), jnp.float32))
        summed = lax.all_gather(column_sum, "rep", axis=1, tiled=True)
        state = update_rows(state, summed, wself, wmid, wout, gain_row)
        results[level].append(state)
    return jnp.stack([jnp.stack(items) for items in results])


def fused_body(sizes, x_ref, code_ref, edst_ref, esrc_ref, ew_ref, wmsg_ref, wself_ref, wmid_ref, wout_ref, gain_ref,
               out_ref, code_v, code_s, edst_v, esrc_v, ew_v, big, ybuf, cbuf, pick0, pick1,
               e_send, e_recv, l_sem, y_send, y_recv, f_send, f_recv, c_send, c_recv):
    rows, width, slots, sections, rep_n, row_n = sizes
    half_rows = rows // 2
    per_half = half_rows // BS
    rep, row, pipe = lax.axis_index("rep"), lax.axis_index("row"), lax.axis_index("pipe")
    other = 1 - pipe

    def at_rep(o):
        return lax.rem(rep + o, rep_n)

    def at_row(o):
        return lax.rem(row + o, row_n)

    barrier = pltpu.get_barrier_semaphore()
    for o in range(1, rep_n):
        pl.semaphore_signal(barrier, inc=1, device_id={"rep": at_rep(o)}, device_id_type=MESH)
    for o in range(1, row_n):
        pl.semaphore_signal(barrier, inc=1, device_id={"row": at_row(o)}, device_id_type=MESH)
    pl.semaphore_signal(barrier, inc=1, device_id={"pipe": other}, device_id_type=MESH)

    lane = lax.broadcasted_iota(jnp.int32, (1, LANES), 1)
    low = lane < HALF

    def project(level, state):
        w = wmsg_ref[level]
        lo = jnp.zeros((width, LANES), jnp.bfloat16)
        hi = lo
        for r in range(rep_n):
            base = (r // 2) * LANES
            w128 = w[:, base:base + LANES]
            rolled = jnp.concatenate([w128[:, HALF:], w128[:, :HALF]], axis=1)
            first, second = (w128, rolled) if r % 2 == 0 else (rolled, w128)
            pick = (rep == r).astype(jnp.float32)
            lo = lo + first * (jnp.where(low, 1.0, 0.0) * pick).astype(jnp.bfloat16)
            hi = hi + second * (jnp.where(low, 0.0, 1.0) * pick).astype(jnp.bfloat16)
        packed = jnp.dot(state[:half_rows], lo, preferred_element_type=jnp.float32)
        packed = packed + jnp.dot(state[half_rows:], hi, preferred_element_type=jnp.float32)
        ybuf[level, pipe * row_n + row] = packed.astype(jnp.bfloat16).reshape(per_half, BS, LANES)

    def y_copy(level, o):
        mine = ybuf.at[level, pipe * row_n + row]
        return pltpu.make_async_remote_copy(mine, mine, y_send.at[level, o], y_recv.at[level, o],
                                            device_id={"row": at_row(o)}, device_id_type=MESH)

    def forward(level, o):
        block = ybuf.at[level, pipe * row_n + at_row(row_n - o)]
        return pltpu.make_async_remote_copy(block, block, f_send.at[level, o], f_recv.at[level, o],
                                            device_id={"pipe": other}, device_id_type=MESH)

    def edge_copies(o):
        made = []
        for i, (src, dst) in enumerate(((code_ref, code_v), (edst_ref, edst_v), (esrc_ref, esrc_v), (ew_ref, ew_v))):
            made.append(pltpu.make_async_remote_copy(src, dst.at[rep], e_send.at[o, i], e_recv.at[o, i],
                                                     device_id={"rep": at_rep(o)}, device_id_type=MESH))
        return made

    local = [pltpu.make_async_copy(src, dst.at[rep], l_sem.at[i]) for i, (src, dst) in enumerate(
        ((code_ref, code_s), (edst_ref, edst_v), (esrc_ref, esrc_v), (ew_ref, ew_v)))]
    for copy in local:
        copy.start()
    project(0, x_ref[...])
    pl.semaphore_wait(barrier, rep_n + row_n - 1)

    def send_y(level):
        forward(level, 0).start()
        for o in range(1, row_n):
            y_copy(level, o).start()

    send_y(0)
    for o in range(1, rep_n):
        for copy in edge_copies(o):
            copy.start()

    rows_a = lax.broadcasted_iota(jnp.int32, (BS, 1), 0)
    rows_b = lax.broadcasted_iota(jnp.int32, (LANES, 1), 0)
    nt = (((1,), (1,)), ((), ()))

    def build(q):
        def section(j, carry):
            s = j * rep_n + q
            for k in range(0, slots, 2):
                total = None
                masks = []
                for h in range(2):
                    d_row = edst_v[q, j, pl.ds(k + h, 1), :]
                    s_row = esrc_v[q, j, pl.ds(k + h, 1), :]
                    w_row = ew_v[q, j, pl.ds(k + h, 1), :]
                    a = jnp.where(rows_a == d_row, w_row, 0.0).astype(jnp.bfloat16)
                    b = jnp.where(rows_b == s_row + h * HALF, 1.0, 0.0).astype(jnp.bfloat16)
                    part = lax.dot_general(a, b, nt, preferred_element_type=jnp.float32)
                    total = part if total is None else total + part
                    masks.append(code_s[q, 0, j * slots + k + h] // 8)
                tile = total.astype(jnp.bfloat16)
                where_to = jnp.where(low, masks[0], masks[1])
                for d in range(rows // BS):
                    keep = jnp.where(where_to == d, 1.0, 0.0).astype(jnp.bfloat16)
                    big[s, d * BS:(d + 1) * BS, k * BS:(k + 2) * BS] = tile * keep
            return carry

        lax.fori_loop(0, sections, section, 0)

    def gathered(level, s, turn):
        pick = pick0 if turn % 2 == 0 else pick1
        pick[...] = ybuf[level, s]
        q = lax.rem(s, rep_n)
        j = s // rep_n
        parts = []
        for k in range(slots):
            src = lax.rem(code_s[q, 0, j * slots + k], 8)
            block = pick[lax.rem(src, per_half)]
            keep = jnp.where(lane // HALF == src // per_half, 1.0, 0.0).astype(jnp.bfloat16)
            parts.append(block * keep)
        return jnp.dot(big[s], jnp.concatenate(parts, axis=0), preferred_element_type=jnp.float32)

    def here(p, o):
        return p * row_n + at_row(row_n - o)

    order = [1, row_n - 1] + list(range(2, row_n - 1)) if row_n > 2 else list(range(1, row_n))

    for copy in local:
        copy.wait()
    build(rep)
    for o in range(1, row_n):
        y_copy(0, o).wait_recv()
        forward(0, o).start()

    def from_peer(o, carry):
        q = at_rep(rep_n - o)
        for copy in edge_copies(o):
            copy.wait_recv()
        fetch = pltpu.make_async_copy(code_v.at[q], code_s.at[q], l_sem.at[4])
        fetch.start()
        fetch.wait()
        build(q)
        return carry

    lax.fori_loop(1, rep_n, from_peer, 0)

    state = x_ref[...]
    for level in range(LAYERS):
        if level > 0:
            project(level, state)
            send_y(level)
        acc = gathered(level, pipe * row_n + row, 0)
        forward(level, 0).wait_recv()
        acc = acc + gathered(level, here(other, 0), 1)
        for o in order:
            if level > 0:
                y_copy(level, o).wait_recv()
                forward(level, o).start()
            acc = acc + gathered(level, here(pipe, o), o + 1)
        for o in order:
            forward(level, o).wait_recv()
            acc = acc + gathered(level, here(other, o), o)
        top, bottom = acc[:half_rows], acc[half_rows:]
        packed = jnp.where(low, top + pltpu.roll(top, HALF, 1), bottom + pltpu.roll(bottom, HALF, 1))
        cbuf[level, rep] = packed.astype(jnp.bfloat16)

        def c_copy(o):
            mine = cbuf.at[level, rep]
            return pltpu.make_async_remote_copy(mine, mine, c_send.at[level, o], c_recv.at[level, o],
                                                device_id={"rep": at_rep(o)}, device_id_type=MESH)

        for o in range(1, rep_n):
            c_copy(o).start()
        own = jnp.dot(state, wself_ref[level], preferred_element_type=jnp.float32)
        for o in range(1, rep_n):
            c_copy(o).wait_recv()
        tops, bottoms = [], []
        for r in range(0, rep_n, 2):
            even = cbuf[level, r].astype(jnp.float32)
            odd = cbuf[level, r + 1].astype(jnp.float32)
            tops.append(jnp.where(low, even, pltpu.roll(odd, HALF, 1)))
            bottoms.append(jnp.where(low, pltpu.roll(even, HALF, 1), odd))
        summed = jnp.concatenate([jnp.concatenate(tops, axis=1), jnp.concatenate(bottoms, axis=1)], axis=0)
        stat = jnp.mean(summed * summed, axis=-1, keepdims=True)
        pre = own + summed * lax.rsqrt(stat + 1e-05) * gain_ref[pl.ds(level, 1), :]
        first = (pre / (1.0 + jnp.exp(-pre))).astype(jnp.bfloat16)
        mid = jnp.dot(first, wmid_ref[level], preferred_element_type=jnp.float32)
        second = (mid / (1.0 + jnp.exp(-mid))).astype(jnp.bfloat16)
        state = (state.astype(jnp.float32)
                 + jnp.dot(second, wout_ref[level], preferred_element_type=jnp.float32)).astype(jnp.bfloat16)
        out_ref[level, 0] = state
        for o in range(1, rep_n):
            c_copy(o).wait_send()
        for o in range(1, row_n):
            y_copy(level, o).wait_send()
        for o in range(row_n):
            forward(level, o).wait_send()
    for o in range(1, rep_n):
        for copy in edge_copies(o):
            copy.wait_send()


def fused(features, tile_src, tile_dst, tile_count, edge_dst, edge_src, edge_weight, w_msg, w_self, w_mid, w_out, gain):
    _, rows, width = features.shape
    sections, slots, edges = edge_dst.shape[2:]
    rep_n, row_n, pipe_n = lax.axis_size("rep"), lax.axis_size("row"), lax.axis_size("pipe")
    groups = row_n * pipe_n
    live = jnp.arange(slots)[None, :] < tile_count[0, 0][:, None]
    code = (tile_src[0, 0] + 8 * jnp.where(live, tile_dst[0, 0], 8)).reshape(1, sections * slots)
    code = jnp.pad(code, ((0, 7), (0, LANES - sections * slots)))
    vmem = pl.BlockSpec(memory_space=pltpu.VMEM)
    dma = pltpu.SemaphoreType.DMA
    return pl.pallas_call(
        functools.partial(fused_body, (rows, width, slots, sections, rep_n, row_n)),
        out_shape=jax.ShapeDtypeStruct((LAYERS, 1, rows, width), jnp.bfloat16),
        in_specs=[vmem] * 10,
        out_specs=vmem,
        scratch_shapes=[
            pltpu.VMEM((rep_n, 8, LANES), jnp.int32),
            pltpu.SMEM((rep_n, 8, LANES), jnp.int32),
            pltpu.VMEM((rep_n, sections, slots, edges), jnp.int32),
            pltpu.VMEM((rep_n, sections, slots, edges), jnp.int32),
            pltpu.VMEM((rep_n, sections, slots, edges), jnp.float32),
            pltpu.VMEM((groups, rows, slots * BS), jnp.bfloat16),
            pltpu.VMEM((LAYERS, groups, rows // BS // 2, BS, LANES), jnp.bfloat16),
            pltpu.VMEM((LAYERS, rep_n, rows // 2, LANES), jnp.bfloat16),
            pltpu.VMEM((rows // BS // 2, BS, LANES), jnp.bfloat16),
            pltpu.VMEM((rows // BS // 2, BS, LANES), jnp.bfloat16),
            dma((rep_n, 4)), dma((rep_n, 4)), dma((5,)),
            dma((LAYERS, row_n)), dma((LAYERS, row_n)),
            dma((LAYERS, row_n)), dma((LAYERS, row_n)),
            dma((LAYERS, rep_n)), dma((LAYERS, rep_n)),
        ],
        compiler_params=pltpu.CompilerParams(
            collective_id=0, has_side_effects=True, vmem_limit_bytes=40 * 1024 * 1024),
    )(features[0], code, edge_dst[0, 0], edge_src[0, 0], edge_weight[0, 0], w_msg, w_self, w_mid, w_out, gain)


def on_device(*args):
    events, rows, width = args[0].shape
    sections, slots = args[4].shape[2:4]
    groups = lax.axis_size("row") * lax.axis_size("pipe")
    rep_n = lax.axis_size("rep")
    fits = (
        events == 1
        and lax.axis_size("pipe") == 2
        and rows // BS == 8
        and width == rep_n * HALF
        and rep_n % 2 == 0
        and sections * rep_n == groups
        and slots % 2 == 0
        and sections * slots <= LANES
        and groups * rows * slots * BS * 2 <= 16 * 1024 * 1024
    )
    return fused(*args) if fits else by_sections(*args)


def solution(mesh):
    placed = (
        P(None, ("pipe", "row"), None),
        P(("pipe", "row"), "rep", None, None),
        P(("pipe", "row"), "rep", None, None),
        P(("pipe", "row"), "rep", None),
        P(("pipe", "row"), "rep", None, None, None),
        P(("pipe", "row"), "rep", None, None, None),
        P(("pipe", "row"), "rep", None, None, None),
        P(),
        P(),
        P(),
        P(),
        P(),
    )
    return jax.shard_map(
        on_device,
        mesh=mesh,
        in_specs=placed,
        out_specs=P(None, None, ("pipe", "row"), None),
        check_vma=False,
    )
```
